32 devices in a mesh: layer: 4 (over y, x), row: 2 (over core), col: 4 (over z).
Axes of the slice: x: 2, y: 2, z: 4, core: 2. Of those that a mesh axis runs over, the one named last changes fastest.
Arguments:
- even_left: bfloat16 [2, 4, 32, 32, 256, 128], P(None, 'layer', 'row', 'col'), may hold values from -0.09375 to 0.09375
- even_right: bfloat16 [2, 4, 32, 32, 256, 128], P(None, 'layer', 'row', 'col'), may hold values from -0.25 to 0.25
- odd_left: bfloat16 [2, 4, 32, 32, 256, 128], P(None, 'layer', 'col', 'row'), may hold values from -0.09375 to 0.09375
- odd_right: bfloat16 [2, 4, 32, 32, 256, 128], P(None, 'layer', 'col', 'row'), may hold values from -0.25 to 0.25
- even_ranks: int32 [2, 4, 32, 32], P(None, 'layer', 'row', 'col'), may hold values from 16 to 64, as said below
- odd_ranks: int32 [2, 4, 32, 32], P(None, 'layer', 'col', 'row'), may hold values from 16 to 64, as said below
- even_sources: float32 [2, 4, 2, 8192, 128], P(None, 'layer', None, ('row', 'col')), may hold values from -6 to 6
- odd_sources: float32 [2, 4, 2, 8192, 128], P(None, 'layer', None, ('col', 'row')), may hold values from -6 to 6
Outputs:
- even_traces: float32 [4, 2, 8192, 128], P('layer', None, ('row', 'col'))
- odd_traces: float32 [4, 2, 8192, 128], P('layer', None, ('col', 'row'))
The draws below stay inside these ranges and needn't reach their ends.
Inputs may be any that keep to these rules, and one draw needn't show every extreme that they name: `even_ranks`: every direction and pair has a tile of rank 64 and a tile of rank a quarter of 64. `odd_ranks`: every direction and pair has a tile of rank 64 and a tile of rank a quarter of 64.
All inputs are finite; a program needn't handle non-finite values.
Results may differ from the reference program's by a relative error of at most 0.008.
Values may be sent and summed in bfloat16 or wider, within the bound.
A program may use at most 256 MiB of HBM per device.

```python
import jax
import jax.numpy as jnp
from jax import lax

NT = 8192
TILE = 256
RMAX = 64
BATCH = 64
NB = 2
TILES = 32
PAIRS = 4
LAYERS = 8


def rank_table(seed_key):
    total = TILES * TILES
    drawn = jax.random.randint(jax.random.fold_in(seed_key, 11), (2, PAIRS, total), RMAX // 4, RMAX + 1)
    top_spot = jax.random.randint(jax.random.fold_in(seed_key, 12), (2, PAIRS, 1), 0, total)
    offset = jax.random.randint(jax.random.fold_in(seed_key, 13), (2, PAIRS, 1), 0, total - 1)
    low_spot = (top_spot + 1 + offset) % total
    places = lax.iota(jnp.int32, total)[None, None, :]
    rank_grid = jnp.where(places == top_spot, RMAX, drawn)
    rank_grid = jnp.where(places == low_spot, RMAX // 4, rank_grid)
    return rank_grid.reshape(2, PAIRS, TILES, TILES).astype(jnp.int32)


def draw_even_ranks(key, part):
    return rank_table(jax.random.fold_in(key, 1))


def draw_odd_ranks(key, part):
    return rank_table(jax.random.fold_in(key, 2))


def shard_levels(key, shape, shards, low, high):
    level, own = 1.0, jax.random.fold_in(key, 6)
    for position, blocks in shards:
        steps = jnp.exp(jax.random.uniform(jax.random.fold_in(own, position), (blocks,), jnp.float32, low / len(shards), high / len(shards)))
        level = level * jnp.repeat(steps, shape[position] // blocks).reshape([-1 if axis == position else 1 for axis in range(len(shape))])
    return level


def centred(key, extent, scale, reach, cuts=(), dtype=jnp.bfloat16):
    array = jax.random.normal(key, extent, jnp.float32) * scale
    if len(cuts) > 0:
        array = shard_levels(key, extent, cuts, -0.22, 0.18) * array
    return jnp.clip(array, min=-reach, max=reach).astype(dtype)


def setup_inputs(seed: int = 0) -> dict:
    arg_keys = jax.random.split(jax.random.key(seed), 9)
    even_left = centred(arg_keys[0], (2, PAIRS, TILES, TILES, TILE, 2 * RMAX), (2 * RMAX * TILES) ** -0.5, 0.09375, ((1, 4), (2, 2), (3, 4)))
    even_right = centred(arg_keys[1], (2, PAIRS, TILES, TILES, TILE, 2 * RMAX), (2 * TILE) ** -0.5, 0.25, ((1, 4), (2, 2), (3, 4)))
    odd_left = centred(arg_keys[2], (2, PAIRS, TILES, TILES, TILE, 2 * RMAX), (2 * RMAX * TILES) ** -0.5, 0.09375, ((1, 4), (2, 4), (3, 2)))
    odd_right = centred(arg_keys[3], (2, PAIRS, TILES, TILES, TILE, 2 * RMAX), (2 * TILE) ** -0.5, 0.25, ((1, 4), (2, 4), (3, 2)))
    even_ranks = draw_even_ranks(jax.random.fold_in(arg_keys[8], 71), 0)
    odd_ranks = draw_odd_ranks(jax.random.fold_in(arg_keys[8], 71), 0)
    even_sources = centred(arg_keys[6], (2, PAIRS, NB, NT, 2 * BATCH), 1.0, 6.0, ((1, 4), (3, 8)), jnp.float32)
    odd_sources = centred(arg_keys[7], (2, PAIRS, NB, NT, 2 * BATCH), 1.0, 6.0, ((1, 4), (3, 8)), jnp.float32)
    return dict(even_left=even_left, even_right=even_right, odd_left=odd_left, odd_right=odd_right, even_ranks=even_ranks, odd_ranks=odd_ranks, even_sources=even_sources, odd_sources=odd_sources)


def tile_product(gathered, left_factor, right_factor, tile_ranks):
    batch_count = gathered.shape[0]
    tile_rows, tile_cols, tile_size, twice_rank = right_factor.shape
    half_rank = twice_rank // 2
    width = gathered.shape[2]
    half_cols = width // 2
    traces = gathered.reshape(batch_count, tile_cols, tile_size, width).astype(jnp.float32)
    products = jnp.einsum('acnr,kcnb->kacrb', right_factor.astype(jnp.float32), traces, preferred_element_type=jnp.float32)
    real_part = products[:, :, :, :half_rank, :half_cols] - products[:, :, :, half_rank:, half_cols:]
    imag_part = products[:, :, :, :half_rank, half_cols:] + products[:, :, :, half_rank:, :half_cols]
    rank_mask = (lax.iota(jnp.int32, half_rank)[None, None, :] < tile_ranks[:, :, None]).astype(jnp.float32)
    rank_mask = rank_mask[None, :, :, :, None]
    real_part = real_part * rank_mask
    imag_part = imag_part * rank_mask
    stacked = jnp.concatenate([jnp.concatenate([real_part, imag_part], axis=4), jnp.concatenate([-imag_part, real_part], axis=4)], axis=3).astype(jnp.bfloat16)
    result = jnp.einsum('acmr,kacrb->kamb', left_factor.astype(jnp.float32), stacked.astype(jnp.float32), preferred_element_type=jnp.float32)
    return result.reshape(batch_count, tile_rows * tile_size, width)


def reference(even_left, even_right, odd_left, odd_right, even_ranks, odd_ranks, even_sources, odd_sources):
    def pick(layer_index, direction):
        pair_index = layer_index // 2
        if layer_index % 2 == 0:
            return even_left[direction, pair_index], even_right[direction, pair_index], even_ranks[direction, pair_index], even_sources[direction, pair_index]
        return odd_left[direction, pair_index], odd_right[direction, pair_index], odd_ranks[direction, pair_index], odd_sources[direction, pair_index]

    down_traces = []
    current = jnp.zeros((NB, NT, 2 * BATCH), jnp.float32)
    for layer_index in range(LAYERS):
        left_factor, right_factor, tile_ranks, sources = pick(layer_index, 0)
        current = tile_product(current.astype(jnp.bfloat16), left_factor, right_factor, tile_ranks) + sources
        down_traces.append(current)
    up_traces = [None] * LAYERS
    current = jnp.zeros((NB, NT, 2 * BATCH), jnp.float32)
    for layer_index in reversed(range(LAYERS)):
        left_factor, right_factor, tile_ranks, sources = pick(layer_index, 1)
        current = tile_product(current.astype(jnp.bfloat16), left_factor, right_factor, tile_ranks) + sources
        up_traces[layer_index] = current
    even_traces = jnp.stack([down_traces[2 * pair_index] + up_traces[2 * pair_index] for pair_index in range(PAIRS)])
    odd_traces = jnp.stack([down_traces[2 * pair_index + 1] + up_traces[2 * pair_index + 1] for pair_index in range(PAIRS)])
    return even_traces, odd_traces
```

```python
import functools

import jax
import jax.numpy as jnp
from jax import lax
from jax.experimental import pallas as pl
from jax.experimental.pallas import tpu as pltpu
from jax.sharding import PartitionSpec as P

MESH = pl.DeviceIdType.MESH
F32, BF16 = jnp.float32, jnp.bfloat16
SKEW = 2


def sizes(right, sources):
    _, _, rows, cols, tile, twice = right.shape
    batches, shard, width = sources.shape[2:]
    return rows, cols, tile, twice, batches, shard, width, min(tile, shard)


def step_of(count):
    return 2 if count % 2 == 0 else 1


def sweep_kernel(
    erank, orank, eleft, eright, oleft, oright, esrc, osrc, eout, oout,
    ev, eu, ov, ou, se, so, a_recv, b_recv, a_send, b_send, part, x_local, x_odd, x_hand, x_even,
    acc, rs_send, rs_recv, hand,
    le_sem, lo_sem, src_sem, as_sem, bs_sem, ar_sem, br_sem, us_sem, ur_sem, hs_sem, hr_sem,
    gs_sem, gr_sem, rss_sem, rsr_sem,
):
    rows_e, cols_e, tile, twice, batches, shard, width, chunk = sizes(eright, esrc)
    rows_o, cols_o = oright.shape[2:4]
    half, batch = twice // 2, width // 2
    q = tile // chunk
    own = shard // chunk
    je, jo = rows_e * q, rows_o * q
    pe, po = step_of(rows_e), step_of(cols_o)
    pr, gc = step_of(rows_o), step_of(cols_e)
    segments, peers, line = (lax.axis_size(axis) for axis in ("layer", "row", "col"))
    p, r, i = (lax.axis_index(axis) for axis in ("layer", "row", "col"))
    first = jnp.where(2 * p <= segments - 1, 0, 1)
    has_e = lambda way: jnp.logical_or(way == 1, p > 0)
    has_o = lambda way: jnp.logical_or(way == 0, p < segments - 1)

    barrier = pltpu.get_barrier_semaphore()
    expect = jnp.int32(peers - 1)
    for k in range(1, peers):
        pl.semaphore_signal(barrier, inc=1, device_id={"row": lax.rem(r + k, peers)}, device_id_type=MESH)
    for axis, at, size in (("col", i, line), ("layer", p, segments)):
        for ok, to in ((at > 0, at - 1), (at < size - 1, at + 1)):

            @pl.when(ok)
            def _(axis=axis, to=to):
                pl.semaphore_signal(barrier, inc=1, device_id={axis: to}, device_id_type=MESH)

            expect = expect + jnp.where(ok, 1, 0)

    def src_copy(parity, way, m):
        ref, buf = ((esrc, se), (osrc, so))[parity]
        return pltpu.make_async_copy(ref.at[way, 0, m], buf.at[way, m], src_sem.at[parity, way, m])

    def load_e(way, t):
        at = pl.ds(t * pe, pe)
        return [
            pltpu.make_async_copy(ref.at[way, 0, at], buf.at[at], le_sem.at[n, t])
            for n, (ref, buf) in enumerate(((eright, ev), (eleft, eu)))
        ]

    def load_o(way, t):
        at = pl.ds(t * po, po)
        return [
            pltpu.make_async_copy(ref.at[way, 0, :, at], buf.at[:, at], lo_sem.at[n, t])
            for n, (ref, buf) in enumerate(((oright, ov), (oleft, ou)))
        ]

    def load_all(which, way):
        load, count = ((load_e, rows_e // pe), (load_o, cols_o // po))[which]

        @pl.loop(0, count)
        def _(t):
            for copy in load(way, t):
                copy.start()

    for parity in range(2):
        for way in range(2):
            for m in range(batches):
                src_copy(parity, way, m).start()
    second = 1 - first
    for turn in range(2):
        for which, has in ((0, has_e), (1, has_o)):
            now = (first == which) if turn == 0 else (first != which)

            @pl.when(now & has(first))
            def _(which=which):
                load_all(which, first)

            @pl.when(now & jnp.logical_not(has(first)) & has(second))
            def _(which=which):
                load_all(which, second)

    pl.semaphore_wait(barrier, expect)

    lane = lax.broadcasted_iota(jnp.int32, (1, twice), 1)
    sign = jnp.where(lane < half, 1.0, -1.0).astype(F32)
    within = jnp.where(lane < half, lane, lane - half)

    def stacked_of(coeff, rank):
        mask = (within < rank).astype(F32)
        top = (coeff[:batch] * sign - pltpu.roll(coeff[batch:], half, 1)) * mask
        low = pltpu.roll(top, half, 1) * (-sign)
        return jnp.concatenate([top, low], axis=0).astype(BF16)

    def tile_of(load, t):
        pieces = [load(t * q + n) for n in range(q)]
        return pieces[0] if q == 1 else jnp.concatenate(pieces, axis=1)

    def source_t(buf, way, m, t):
        return buf[way, m, pl.ds(pl.multiple_of(t * chunk, chunk), chunk), :].T

    def keep(out, turn, m, t, value):
        at = pl.ds(pl.multiple_of(t * chunk, chunk), chunk)

        @pl.when(turn == 0)
        def _():
            out[0, m, at, :] = value.T

        @pl.when(turn != 0)
        def _():
            out[0, m, at, :] = out[0, m, at, :] + value.T

    def even_product(way, m, a):
        stacked = [[] for _ in range(pe)]
        for c in range(cols_e):
            right = jnp.concatenate([ev[a + j, c] for j in range(pe)], axis=1)
            x = tile_of(lambda n: x_even[way, m, n], c)
            coeff = jnp.dot(x, right, preferred_element_type=F32)
            for j in range(pe):
                rank = erank[(way * rows_e + a + j) * cols_e + c]
                stacked[j].append(stacked_of(coeff[:, j * twice : (j + 1) * twice], rank))
        for j in range(pe):
            total = lax.dot_general(
                jnp.concatenate(stacked[j], axis=1),
                jnp.concatenate([eu[a + j, c] for c in range(cols_e)], axis=1),
                (((1,), (1,)), ((), ())),
                preferred_element_type=F32,
            )
            for n in range(q):
                part[(a + j) * q + n] = total[:, n * chunk : (n + 1) * chunk]

    def odd_product(way, c, load):
        xs = [tile_of(load, c + g) for g in range(po)]
        for a in range(0, rows_o, pr):
            stacked = [[] for _ in range(pr)]
            for g in range(po):
                right = jnp.concatenate([ov[a + j, c + g] for j in range(pr)], axis=1)
                coeff = jnp.dot(xs[g], right, preferred_element_type=F32)
                for j in range(pr):
                    rank = orank[(way * rows_o + a + j) * cols_o + c + g]
                    stacked[j].append(stacked_of(coeff[:, j * twice : (j + 1) * twice], rank))
            for j in range(pr):
                total = lax.dot_general(
                    jnp.concatenate(stacked[j], axis=1),
                    jnp.concatenate([ou[a + j, c + g] for g in range(po)], axis=1),
                    (((1,), (1,)), ((), ())),
                    preferred_element_type=F32,
                )
                for n in range(q):
                    at = (a + j) * q + n
                    acc[at] = acc[at] + total[:, n * chunk : (n + 1) * chunk]

    def a_copy(k, j):
        return pltpu.make_async_remote_copy(
            src_ref=a_send.at[j], dst_ref=a_recv.at[k, j],
            send_sem=as_sem.at[j], recv_sem=ar_sem.at[k, j],
            device_id={"col": lax.rem(i + 1, line)}, device_id_type=MESH,
        )

    def b_copy(k, j):
        return pltpu.make_async_remote_copy(
            src_ref=b_send.at[j], dst_ref=b_recv.at[k, j],
            send_sem=bs_sem.at[j], recv_sem=br_sem.at[k, j],
            device_id={"col": lax.rem(i + line - 1, line)}, device_id_type=MESH,
        )

    def up_copy(m, j):
        return pltpu.make_async_remote_copy(
            src_ref=x_hand.at[j], dst_ref=x_odd.at[m, j],
            send_sem=us_sem.at[j], recv_sem=ur_sem.at[m, j],
            device_id={"layer": lax.rem(p + segments - 1, segments)}, device_id_type=MESH,
        )

    def down_copy(m, t):
        return pltpu.make_async_remote_copy(
            src_ref=hand.at[t], dst_ref=x_even.at[0, m, r * own + t],
            send_sem=hs_sem.at[t], recv_sem=hr_sem.at[m, t],
            device_id={"layer": lax.rem(p + 1, segments)}, device_id_type=MESH,
        )

    def gather_copy(k, way, m, t, d, source):
        slot = x_even.at[way, m, source * own + t]
        return pltpu.make_async_remote_copy(
            src_ref=slot, dst_ref=slot,
            send_sem=gs_sem.at[d - 1, t], recv_sem=gr_sem.at[k, d - 1, t],
            device_id={"row": lax.rem(r + d, peers)}, device_id_type=MESH,
        )

    def scatter_copy(k, d):
        return pltpu.make_async_remote_copy(
            src_ref=rs_send.at[d - 1], dst_ref=rs_recv.at[k, d - 1],
            send_sem=rss_sem.at[d - 1], recv_sem=rsr_sem.at[k, d - 1],
            device_id={"row": lax.rem(r + d, peers)}, device_id_type=MESH,
        )

    def even_part(way, k, turn, m):
        full = has_e(way)
        final = jnp.logical_and(way == 1, p == 0)

        def sends_a(at, o):
            need = jnp.logical_or(full, at >= o) & (jnp.logical_not(final) | (o > at))
            return need & (at >= 0) & (at < line - 1)

        def sends_b(at, o):
            need = jnp.logical_or(full, at <= o) & (jnp.logical_not(final) | (o < at))
            return need & (at > 0) & (at < line)

        src_copy(0, way, m).wait()

        @pl.when(full)
        def _():
            for t in range(own):
                if way == 0:
                    down_copy(m, t).wait_recv()
                for d in range(1, peers):
                    gather_copy(k, way, m, t, d, r).start()
            for t in range(own):
                for d in range(1, peers):
                    gather_copy(k, way, m, t, d, lax.rem(r + peers - d, peers)).wait_recv()

        @pl.when(jnp.logical_not(full))
        def _():
            @pl.loop(0, je)
            def _(j):
                part[j] = jnp.zeros((width, chunk), F32)

            for t in range(own):
                part[i * own + t] = source_t(se, way, m, t)

        behind = jnp.maximum(i, line - 1 - i)

        @pl.loop(0, je + SKEW * (line - 1))
        def _(s):
            @pl.when(full & (s < je) & (lax.rem(s, pe * q) == 0))
            def _():
                t = s // (pe * q)

                @pl.when(m == 0)
                def _():
                    for copy in load_e(way, t):
                        copy.wait()

                even_product(way, m, t * pe)

                @pl.when((k == batches - 1) & has_e(second))
                def _():
                    for copy in load_e(second, t):
                        copy.start()

                for n in range(pe * q):
                    mine = s + n - i * own

                    @pl.when((mine >= 0) & (mine < own))
                    def _(n=n, mine=mine):
                        part[s + n] = part[s + n] + source_t(se, way, m, mine)

            ja = s - SKEW * i

            @pl.when((ja >= 0) & (ja < je))
            def _():
                o = ja // own
                got, put = sends_a(i - 1, o), sends_a(i, o)

                @pl.when(got)
                def _():
                    a_copy(k, ja).wait_recv()

                @pl.when(put & got)
                def _():
                    a_send[ja] = (part[ja] + a_recv[k, ja].astype(F32)).astype(BF16)

                @pl.when(put & jnp.logical_not(got))
                def _():
                    a_send[ja] = part[ja].astype(BF16)

                @pl.when(put)
                def _():
                    a_copy(k, ja).start()

            jb = s - SKEW * (line - 1 - i)

            @pl.when((jb >= 0) & (jb < je))
            def _():
                o = jb // own
                got, put = sends_b(i + 1, o), sends_b(i, o)

                @pl.when(got)
                def _():
                    b_copy(k, jb).wait_recv()

                @pl.when(put & got)
                def _():
                    b_send[jb] = (part[jb] + b_recv[k, jb].astype(F32)).astype(BF16)

                @pl.when(put & jnp.logical_not(got))
                def _():
                    b_send[jb] = part[jb].astype(BF16)

                @pl.when(put)
                def _():
                    b_copy(k, jb).start()

            jt = s - SKEW * behind

            @pl.when((jt >= 0) & (jt < je))
            def _():
                o = jt // own
                mine = o == i

                @pl.when(jnp.logical_not(final) | mine)
                def _():
                    @pl.when(sends_a(i - 1, o))
                    def _():
                        part[jt] = part[jt] + a_recv[k, jt].astype(F32)

                    @pl.when(sends_b(i + 1, o))
                    def _():
                        part[jt] = part[jt] + b_recv[k, jt].astype(F32)

                @pl.when(mine)
                def _():
                    keep(eout, turn, m, jt - i * own, part[jt])

                if way == 0:
                    x_local[jt] = part[jt].astype(BF16)

                    @pl.when(lax.rem(jt, po * q) == po * q - 1)
                    def _():
                        odd_columns(way, k, m, jt // (po * q), lambda n: x_local[n])

                else:

                    @pl.when(jnp.logical_not(final))
                    def _():
                        x_hand[jt] = part[jt].astype(BF16)
                        up_copy(m, jt).start()

        @pl.when(full)
        def _():
            for t in range(own):
                for d in range(1, peers):
                    gather_copy(k, way, m, t, d, r).wait_send()

        @pl.loop(0, je)
        def _(j):
            o = j // own

            @pl.when(sends_a(i, o))
            def _():
                a_copy(k, j).wait_send()

            @pl.when(sends_b(i, o))
            def _():
                b_copy(k, j).wait_send()

            if way == 1:

                @pl.when(jnp.logical_not(final))
                def _():
                    up_copy(m, j).wait_send()

    def odd_columns(way, k, m, t, load):
        @pl.when(m == 0)
        def _():
            for copy in load_o(way, t):
                copy.wait()

        @pl.when(t == 0)
        def _():
            @pl.loop(0, jo)
            def _(j):
                acc[j] = jnp.zeros((width, chunk), F32)

        odd_product(way, t * po, load)

        @pl.when((k == batches - 1) & has_o(second))
        def _():
            for copy in load_o(second, t):
                copy.start()

    def odd_rest(way, k, turn, m):
        full = has_o(way)
        src_copy(1, way, m).wait()

        @pl.when(full)
        def _():
            for d in range(1, peers):
                target = lax.rem(r + d, peers)
                for t in range(own):
                    rs_send[d - 1, t] = acc[target * own + t].astype(BF16)
                scatter_copy(k, d).start()
            for d in range(1, peers):
                scatter_copy(k, d).wait_recv()
                for t in range(own):
                    at = r * own + t
                    acc[at] = acc[at] + rs_recv[k, d - 1, t].astype(F32)

        @pl.when(jnp.logical_not(full))
        def _():
            for t in range(own):
                acc[r * own + t] = jnp.zeros((width, chunk), F32)

        for t in range(own):
            at = r * own + t
            total = acc[at] + source_t(so, way, m, t)
            if way == 0:

                @pl.when(p < segments - 1)
                def _(t=t, total=total):
                    hand[t] = total.astype(BF16)
                    down_copy(m, t).start()

            else:
                x_even[way, m, at] = total.astype(BF16)
            keep(oout, turn, m, t, total)

        @pl.when(full)
        def _():
            for d in range(1, peers):
                scatter_copy(k, d).wait_send()

        if way == 0:

            @pl.when(p < segments - 1)
            def _():
                for t in range(own):
                    down_copy(m, t).wait_send()

    @pl.loop(0, 2 * batches)
    def _(k):
        turn, m = k // batches, lax.rem(k, batches)
        way = jnp.where(turn == 0, first, second)

        @pl.when(way == 0)
        def _():
            even_part(0, k, turn, m)
            odd_rest(0, k, turn, m)

        @pl.when(way == 1)
        def _():
            @pl.when(has_o(1))
            def _():
                @pl.loop(0, cols_o // po)
                def _(t):
                    for n in range(po * q):
                        up_copy(m, t * po * q + n).wait_recv()
                    odd_columns(1, k, m, t, lambda n: x_odd[m, n])

            odd_rest(1, k, turn, m)
            even_part(1, k, turn, m)


def on_device(even_left, even_right, odd_left, odd_right, even_ranks, odd_ranks, even_sources, odd_sources):
    rows_e, cols_e, tile, twice, batches, shard, width, chunk = sizes(even_right, even_sources)
    rows_o, cols_o = odd_right.shape[2:4]
    peers = lax.axis_size("row")
    q, own, stages = tile // chunk, shard // chunk, 2 * batches
    je, jo, others = rows_e * q, rows_o * q, max(peers - 1, 1)
    hbm = pl.BlockSpec(memory_space=pltpu.HBM)
    smem = pl.BlockSpec(memory_space=pltpu.SMEM)
    vmem = pl.BlockSpec(memory_space=pltpu.VMEM)
    dma = lambda *shape: pltpu.SemaphoreType.DMA(shape)
    piece = (width, chunk)
    out = jax.ShapeDtypeStruct((1, batches, shard, width), F32)
    scratch = [
        pltpu.VMEM((rows_e, cols_e, tile, twice), BF16),
        pltpu.VMEM((rows_e, cols_e, tile, twice), BF16),
        pltpu.VMEM((rows_o, cols_o, tile, twice), BF16),
        pltpu.VMEM((rows_o, cols_o, tile, twice), BF16),
        pltpu.VMEM((2, batches, shard, width), F32),
        pltpu.VMEM((2, batches, shard, width), F32),
        pltpu.VMEM((stages, je) + piece, BF16),
        pltpu.VMEM((stages, je) + piece, BF16),
        pltpu.VMEM((je,) + piece, BF16),
        pltpu.VMEM((je,) + piece, BF16),
        pltpu.VMEM((je,) + piece, F32),
        pltpu.VMEM((je,) + piece, BF16),
        pltpu.VMEM((batches, je) + piece, BF16),
        pltpu.VMEM((je,) + piece, BF16),
        pltpu.VMEM((2, batches, jo) + piece, BF16),
        pltpu.VMEM((jo,) + piece, F32),
        pltpu.VMEM((others, own) + piece, BF16),
        pltpu.VMEM((stages, others, own) + piece, BF16),
        pltpu.VMEM((own,) + piece, BF16),
        dma(2, rows_e // step_of(rows_e)),
        dma(2, cols_o // step_of(cols_o)),
        dma(2, 2, batches),
        dma(je),
        dma(je),
        dma(stages, je),
        dma(stages, je),
        dma(je),
        dma(batches, je),
        dma(own),
        dma(batches, own),
        dma(others, own),
        dma(stages, others, own),
        dma(others),
        dma(stages, others),
    ]
    return pl.pallas_call(
        sweep_kernel,
        out_shape=[out, out],
        in_specs=[smem] * 2 + [hbm] * 6,
        out_specs=[vmem] * 2,
        scratch_shapes=scratch,
        compiler_params=pltpu.CompilerParams(
            collective_id=0,
            has_side_effects=True,
            vmem_limit_bytes=63 * 1024 * 1024,
        ),
        name="sweep",
    )(
        even_ranks.reshape(-1),
        odd_ranks.reshape(-1),
        even_left,
        even_right,
        odd_left,
        odd_right,
        even_sources,
        odd_sources,
    )


def solution(mesh):
    in_specs = (
        P(None, "layer", "row", "col", None, None),
        P(None, "layer", "row", "col", None, None),
        P(None, "layer", "col", "row", None, None),
        P(None, "layer", "col", "row", None, None),
        P(None, "layer", "row", "col"),
        P(None, "layer", "col", "row"),
        P(None, "layer", None, ("row", "col"), None),
        P(None, "layer", None, ("col", "row"), None),
    )
    out_specs = (P("layer", None, ("row", "col"), None), P("layer", None, ("col", "row"), None))
    return jax.shard_map(
        on_device, mesh=mesh, in_specs=in_specs, out_specs=out_specs, check_vma=False
    )
```

```python
import functools

import jax
import jax.numpy as jnp
from jax import lax
from jax.experimental import pallas as pl
from jax.experimental.pallas import tpu as pltpu
from jax.sharding import PartitionSpec as P

MESH = pl.DeviceIdType.MESH
F32, BF16 = jnp.float32, jnp.bfloat16


def sizes(right, sources):
    _, _, rows, cols, tile, twice = right.shape
    batches, shard, width = sources.shape[2:]
    return rows, cols, tile, twice, batches, shard, width, min(tile, shard)


def step_of(count):
    return 2 if count % 2 == 0 else 1


def skew_of(count, line):
    return max(1, min(4, (count - 2) // max(line - 1, 1)))


def buffers_of(count, step, line, batches):
    return 1 if skew_of(count, line) * (line - 1) <= count - step else 2, 2 if batches <= 2 else 2 * batches


def sweep_kernel(
    erank, orank, eleft, eright, oleft, oright, esrc, osrc, eout, oout,
    ev, eu, ov, ou, se, so, a_recv, b_recv, a_send, b_send, part, x_local, x_odd, x_hand, x_even,
    stk, acc, rs_send, rs_recv, hand,
    le_sem, lv_sem, lu_sem, src_sem, as_sem, bs_sem, ar_sem, br_sem, us_sem, ur_sem, hs_sem, hr_sem,
    gs_sem, gr_sem, rss_sem, rsr_sem,
):
    rows_e, cols_e, tile, twice, batches, shard, width, chunk = sizes(eright, esrc)
    rows_o, cols_o = oright.shape[2:4]
    half, batch = twice // 2, width // 2
    q = tile // chunk
    own = shard // chunk
    je, jo = rows_e * q, rows_o * q
    pe, po = step_of(rows_e), step_of(cols_o)
    pr = step_of(rows_o)
    segments, peers, line = (lax.axis_size(axis) for axis in ("layer", "row", "col"))
    p, r, i = (lax.axis_index(axis) for axis in ("layer", "row", "col"))
    skew, lag, ends = skew_of(je, line), 2 * po * q, batches * je
    parts, sides = buffers_of(je, pe * q, line, batches)
    first = jnp.where(2 * p <= segments - 1, 0, 1)
    has_e = lambda way: jnp.logical_or(way == 1, p > 0)
    has_o = lambda way: jnp.logical_or(way == 0, p < segments - 1)

    barrier = pltpu.get_barrier_semaphore()
    expect = jnp.int32(peers - 1)
    for k in range(1, peers):
        pl.semaphore_signal(barrier, inc=1, device_id={"row": lax.rem(r + k, peers)}, device_id_type=MESH)
    for axis, at, size in (("col", i, line), ("layer", p, segments)):
        for ok, to in ((at > 0, at - 1), (at < size - 1, at + 1)):

            @pl.when(ok)
            def _(axis=axis, to=to):
                pl.semaphore_signal(barrier, inc=1, device_id={axis: to}, device_id_type=MESH)

            expect = expect + jnp.where(ok, 1, 0)

    def src_copy(parity, way, m):
        ref, buf = ((esrc, se), (osrc, so))[parity]
        return pltpu.make_async_copy(ref.at[way, 0, m], buf.at[way, m], src_sem.at[parity, way, m])

    def load_e(way, t):
        at = pl.ds(t * pe, pe)
        return [
            pltpu.make_async_copy(ref.at[way, 0, at], buf.at[at], le_sem.at[n, t])
            for n, (ref, buf) in enumerate(((eright, ev), (eleft, eu)))
        ]

    def load_v(way, t):
        at = pl.ds(t * po, po)
        return pltpu.make_async_copy(oright.at[way, 0, :, at], ov.at[:, at], lv_sem.at[t])

    def load_u(way, t):
        at = pl.ds(t * pr, pr)
        return pltpu.make_async_copy(oleft.at[way, 0, at], ou.at[at], lu_sem.at[t])

    def load_all(which, way):
        if which == 0:

            @pl.loop(0, rows_e // pe)
            def _(t):
                for copy in load_e(way, t):
                    copy.start()

        else:

            @pl.loop(0, cols_o // po)
            def _(t):
                load_v(way, t).start()

            @pl.loop(0, rows_o // pr)
            def _(t):
                load_u(way, t).start()

    for parity in range(2):
        for way in range(2):
            for m in range(batches):
                src_copy(parity, way, m).start()
    second = 1 - first
    for turn in range(2):
        for which, has in ((0, has_e), (1, has_o)):
            now = (first == which) if turn == 0 else (first != which)

            @pl.when(now & has(first))
            def _(which=which):
                load_all(which, first)

            @pl.when(now & jnp.logical_not(has(first)) & has(second))
            def _(which=which):
                load_all(which, second)

    pl.semaphore_wait(barrier, expect)

    lane = lax.broadcasted_iota(jnp.int32, (1, twice), 1)
    sign = jnp.where(lane < half, 1.0, -1.0).astype(F32)
    within = jnp.where(lane < half, lane, lane - half)

    def stacked_of(coeff, rank):
        mask = (within < rank).astype(F32)
        top = (coeff[:batch] * sign - pltpu.roll(coeff[batch:], half, 1)) * mask
        low = pltpu.roll(top, half, 1) * (-sign)
        return jnp.concatenate([top, low], axis=0).astype(BF16)

    def tile_of(load, t):
        pieces = [load(t * q + n) for n in range(q)]
        return pieces[0] if q == 1 else jnp.concatenate(pieces, axis=1)

    def source_t(buf, way, m, t):
        return buf[way, m, pl.ds(pl.multiple_of(t * chunk, chunk), chunk), :].T

    def keep(out, turn, m, t, value):
        at = pl.ds(pl.multiple_of(t * chunk, chunk), chunk)

        @pl.when(turn == 0)
        def _():
            out[0, m, at, :] = value.T

        @pl.when(turn != 0)
        def _():
            out[0, m, at, :] = out[0, m, at, :] + value.T

    def even_product(way, m, a):
        stacked = [[] for _ in range(pe)]
        for c in range(cols_e):
            right = jnp.concatenate([ev[a + j, c] for j in range(pe)], axis=1)
            x = tile_of(lambda n: x_even[way, m, n], c)
            coeff = jnp.dot(x, right, preferred_element_type=F32)
            for j in range(pe):
                rank = erank[(way * rows_e + a + j) * cols_e + c]
                stacked[j].append(stacked_of(coeff[:, j * twice : (j + 1) * twice], rank))
        for j in range(pe):
            total = lax.dot_general(
                jnp.concatenate(stacked[j], axis=1),
                jnp.concatenate([eu[a + j, c] for c in range(cols_e)], axis=1),
                (((1,), (1,)), ((), ())),
                preferred_element_type=F32,
            )
            for n in range(q):
                part[lax.rem(m, parts), (a + j) * q + n] = total[:, n * chunk : (n + 1) * chunk]

    def odd_columns(way, k, m, t, load):
        @pl.when(m == 0)
        def _():
            load_v(way, t).wait()

        for g in range(po):
            c = t * po + g
            x = tile_of(load, c)
            for a in range(0, rows_o, pr):
                right = jnp.concatenate([ov[a + j, c] for j in range(pr)], axis=1)
                coeff = jnp.dot(x, right, preferred_element_type=F32)
                for j in range(pr):
                    rank = orank[(way * rows_o + a + j) * cols_o + c]
                    stk[way, a + j, c] = stacked_of(coeff[:, j * twice : (j + 1) * twice], rank)

        @pl.when((k == batches - 1) & has_o(second))
        def _():
            load_v(second, t).start()

    def a_copy(k, j):
        return pltpu.make_async_remote_copy(
            src_ref=a_send.at[j], dst_ref=a_recv.at[lax.rem(k, sides), j],
            send_sem=as_sem.at[j], recv_sem=ar_sem.at[lax.rem(k, sides), j],
            device_id={"col": lax.rem(i + 1, line)}, device_id_type=MESH,
        )

    def b_copy(k, j):
        return pltpu.make_async_remote_copy(
            src_ref=b_send.at[j], dst_ref=b_recv.at[lax.rem(k, sides), j],
            send_sem=bs_sem.at[j], recv_sem=br_sem.at[lax.rem(k, sides), j],
            device_id={"col": lax.rem(i + line - 1, line)}, device_id_type=MESH,
        )

    def up_copy(m, j):
        return pltpu.make_async_remote_copy(
            src_ref=x_hand.at[j], dst_ref=x_odd.at[m, j],
            send_sem=us_sem.at[j], recv_sem=ur_sem.at[m, j],
            device_id={"layer": lax.rem(p + segments - 1, segments)}, device_id_type=MESH,
        )

    def down_copy(m, t):
        return pltpu.make_async_remote_copy(
            src_ref=hand.at[t], dst_ref=x_even.at[0, m, r * own + t],
            send_sem=hs_sem.at[t], recv_sem=hr_sem.at[m, t],
            device_id={"layer": lax.rem(p + 1, segments)}, device_id_type=MESH,
        )

    def gather_copy(k, way, m, t, d, source):
        slot = x_even.at[way, m, source * own + t]
        return pltpu.make_async_remote_copy(
            src_ref=slot, dst_ref=slot,
            send_sem=gs_sem.at[d - 1, t], recv_sem=gr_sem.at[k, d - 1, t],
            device_id={"row": lax.rem(r + d, peers)}, device_id_type=MESH,
        )

    def scatter_copy(k, at, d):
        return pltpu.make_async_remote_copy(
            src_ref=rs_send.at[at], dst_ref=rs_recv.at[k, d - 1, lax.rem(at, own)],
            send_sem=rss_sem.at[at], recv_sem=rsr_sem.at[k, d - 1, lax.rem(at, own)],
            device_id={"row": lax.rem(r + d, peers)}, device_id_type=MESH,
        )

    across = (first == 0) & (2 * (p + 1) > segments - 1) & (p < segments - 1)
    behind = jnp.maximum(i, line - 1 - i)

    def sweep_pass(way, turn):
        full = has_e(way)
        final = jnp.logical_and(way == 1, p == 0)
        base = turn * batches

        def sends_a(at, o):
            need = jnp.logical_or(full, at >= o) & (jnp.logical_not(final) | (o > at))
            return need & (at >= 0) & (at < line - 1)

        def sends_b(at, o):
            need = jnp.logical_or(full, at <= o) & (jnp.logical_not(final) | (o < at))
            return need & (at > 0) & (at < line)

        def opening(m):
            k = base + m
            src_copy(0, way, m).wait()
            if way == 1:
                odd_rest(1, k, turn, m)

            @pl.when(full)
            def _():
                for t in range(own):
                    if way == 0:
                        down_copy(m, t).wait_recv()
                        for d in range(1, peers):
                            gather_copy(k, way, m, t, d, r).start()
                if way == 1:
                    keep_odd(turn, m)
                for t in range(own):
                    for d in range(1, peers):
                        gather_copy(k, way, m, t, d, lax.rem(r + peers - d, peers)).wait_recv()
                for t in range(own):
                    for d in range(1, peers):
                        gather_copy(k, way, m, t, d, r).wait_send()

        @pl.loop(0, ends + skew * (line - 1) + lag)
        def _(s):
            @pl.when(s < ends)
            def _():
                m, j = s // je, lax.rem(s, je)
                page = lax.rem(m, parts)

                @pl.when(j == 0)
                def _():
                    opening(m)

                @pl.when(full & (lax.rem(j, pe * q) == 0))
                def _():
                    t = j // (pe * q)

                    @pl.when(m == 0)
                    def _():
                        for copy in load_e(way, t):
                            copy.wait()

                    even_product(way, m, t * pe)

                    @pl.when((turn == 0) & (m == batches - 1) & has_e(second))
                    def _():
                        for copy in load_e(second, t):
                            copy.start()

                    for n in range(pe * q):
                        mine = j + n - i * own

                        @pl.when((mine >= 0) & (mine < own))
                        def _(n=n, mine=mine):
                            part[page, j + n] = part[page, j + n] + source_t(se, way, m, mine)

                @pl.when(jnp.logical_not(full))
                def _():
                    mine = j - i * own
                    part[page, j] = jnp.zeros((width, chunk), F32)

                    @pl.when((mine >= 0) & (mine < own))
                    def _():
                        part[page, j] = source_t(se, way, m, mine)

            ga = s - skew * i

            @pl.when((ga >= 0) & (ga < ends))
            def _():
                m, j = ga // je, lax.rem(ga, je)
                k, page, o = base + m, lax.rem(m, parts), j // own
                got, put = sends_a(i - 1, o), sends_a(i, o)

                @pl.when(got)
                def _():
                    a_copy(k, j).wait_recv()

                @pl.when(put & (m > 0))
                def _():
                    a_copy(k - 1, j).wait_send()

                @pl.when(put & got)
                def _():
                    a_send[j] = (part[page, j] + a_recv[lax.rem(k, sides), j].astype(F32)).astype(BF16)

                @pl.when(put & jnp.logical_not(got))
                def _():
                    a_send[j] = part[page, j].astype(BF16)

                @pl.when(put)
                def _():
                    a_copy(k, j).start()

            gb = s - skew * (line - 1 - i)

            @pl.when((gb >= 0) & (gb < ends))
            def _():
                m, j = gb // je, lax.rem(gb, je)
                k, page, o = base + m, lax.rem(m, parts), j // own
                got, put = sends_b(i + 1, o), sends_b(i, o)

                @pl.when(got)
                def _():
                    b_copy(k, j).wait_recv()

                @pl.when(put & (m > 0))
                def _():
                    b_copy(k - 1, j).wait_send()

                @pl.when(put & got)
                def _():
                    b_send[j] = (part[page, j] + b_recv[lax.rem(k, sides), j].astype(F32)).astype(BF16)

                @pl.when(put & jnp.logical_not(got))
                def _():
                    b_send[j] = part[page, j].astype(BF16)

                @pl.when(put)
                def _():
                    b_copy(k, j).start()

            gt = s - skew * behind

            @pl.when((gt >= 0) & (gt < ends))
            def _():
                m, j = gt // je, lax.rem(gt, je)
                k, page, o = base + m, lax.rem(m, parts), j // own
                mine = o == i

                @pl.when(jnp.logical_not(final) | mine)
                def _():
                    @pl.when(sends_a(i - 1, o))
                    def _():
                        part[page, j] = part[page, j] + a_recv[lax.rem(k, sides), j].astype(F32)

                    @pl.when(sends_b(i + 1, o))
                    def _():
                        part[page, j] = part[page, j] + b_recv[lax.rem(k, sides), j].astype(F32)

                if way == 1:

                    @pl.when(jnp.logical_not(final))
                    def _():
                        @pl.when(m > 0)
                        def _():
                            up_copy(m - 1, j).wait_send()

                        x_hand[j] = part[page, j].astype(BF16)
                        up_copy(m, j).start()

                @pl.when(mine)
                def _():
                    keep(eout, turn, m, j - i * own, part[page, j])

                if way == 0:

                    @pl.when(j == 0)
                    def _():
                        odd_start(0, m)

                    x_local[lax.rem(j, po * q)] = part[page, j].astype(BF16)

                    @pl.when(lax.rem(j, po * q) == po * q - 1)
                    def _():
                        odd_columns(way, k, m, j // (po * q), lambda n: x_local[lax.rem(n, po * q)])

                    @pl.when(j == je - 1)
                    def _():
                        odd_rest(0, k, turn, m)
                        keep_odd(turn, m)

                else:

                    @pl.when((j == 0) & (m < batches - 1))
                    def _():
                        odd_start(1, m + 1)

            if way == 0:
                ju = gt - lag - (batches - 1) * je

                @pl.when((turn == 0) & across & (ju >= 0) & (ju < je) & (lax.rem(ju + je, po * q) == po * q - 1))
                def _():
                    up_columns(base + batches, 0, ju // (po * q))

            else:
                j = lax.rem(s, je)

                @pl.when(has_o(1) & (s < ends - je) & (lax.rem(j, po * q) == po * q - 1))
                def _():
                    up_columns(base + s // je + 1, s // je + 1, j // (po * q))

        last = base + batches - 1

        @pl.loop(0, je)
        def _(j):
            o = j // own

            @pl.when(sends_a(i, o))
            def _():
                a_copy(last, j).wait_send()

            @pl.when(sends_b(i, o))
            def _():
                b_copy(last, j).wait_send()

            if way == 1:

                @pl.when(jnp.logical_not(final))
                def _():
                    up_copy(batches - 1, j).wait_send()

        if way == 0:

            @pl.when(p < segments - 1)
            def _():
                for t in range(own):
                    down_copy(batches - 1, t).wait_send()

    def keep_odd(turn, m):
        for t in range(own):
            keep(oout, turn, m, t, acc[t])

    def up_columns(k, m, t):
        for n in range(po * q):
            up_copy(m, t * po * q + n).wait_recv()
        odd_columns(1, k, m, t, lambda n: x_odd[m, n])

    def odd_start(way, m):
        src_copy(1, way, m).wait()
        for t in range(own):
            acc[t] = source_t(so, way, m, t)

    def odd_rest(way, k, turn, m):
        full = has_o(way)
        begin = (lax.rem(r + 1, peers) * own // (q * pr)) * pr

        @pl.when(full)
        def _():
            @pl.loop(0, rows_o // pr)
            def _(n):
                a = lax.rem(begin + n * pr, rows_o)

                @pl.when(m == 0)
                def _():
                    load_u(way, a // pr).wait()

                totals = [
                    lax.dot_general(
                        jnp.concatenate([stk[way, a + j, c] for c in range(cols_o)], axis=1),
                        jnp.concatenate([ou[a + j, c] for c in range(cols_o)], axis=1),
                        (((1,), (1,)), ((), ())),
                        preferred_element_type=F32,
                    )
                    for j in range(pr)
                ]
                for j in range(pr):
                    for h in range(q):
                        at = (a + j) * q + h
                        owner = at // own
                        value = totals[j][:, h * chunk : (h + 1) * chunk]

                        @pl.when(owner == r)
                        def _(at=at, value=value):
                            mine = at - r * own
                            acc[mine] = acc[mine] + value

                        @pl.when(owner != r)
                        def _(at=at, owner=owner, value=value):
                            rs_send[at] = value.astype(BF16)
                            scatter_copy(k, at, lax.rem(owner + peers - r, peers)).start()

                @pl.when((k == batches - 1) & has_o(second))
                def _():
                    load_u(second, a // pr).start()

            for t in range(own):
                for d in range(1, peers):
                    scatter_copy(k, r * own + t, d).wait_recv()
                    acc[t] = acc[t] + rs_recv[k, d - 1, t].astype(F32)

        for t in range(own):
            if way == 0:

                @pl.when(p < segments - 1)
                def _(t=t):
                    @pl.when(m > 0)
                    def _():
                        down_copy(m - 1, t).wait_send()

                    hand[t] = acc[t].astype(BF16)
                    down_copy(m, t).start()

            else:
                x_even[way, m, r * own + t] = acc[t].astype(BF16)
                for d in range(1, peers):
                    gather_copy(k, way, m, t, d, r).start()

        @pl.when(full)
        def _():
            @pl.loop(0, jo)
            def _(at):
                owner = at // own

                @pl.when(owner != r)
                def _():
                    scatter_copy(k, at, lax.rem(owner + peers - r, peers)).wait_send()

    @pl.loop(0, 2)
    def _(turn):
        way = jnp.where(turn == 0, first, second)

        @pl.when(way == 0)
        def _():
            sweep_pass(0, turn)

        @pl.when(way == 1)
        def _():
            odd_start(1, 0)

            @pl.when(has_o(1) & ((turn == 0) | jnp.logical_not(across)))
            def _():
                @pl.loop(0, cols_o // po)
                def _(t):
                    up_columns(turn * batches, 0, t)

            sweep_pass(1, turn)


def on_device(even_left, even_right, odd_left, odd_right, even_ranks, odd_ranks, even_sources, odd_sources):
    rows_e, cols_e, tile, twice, batches, shard, width, chunk = sizes(even_right, even_sources)
    rows_o, cols_o = odd_right.shape[2:4]
    peers = lax.axis_size("row")
    q, own, stages = tile // chunk, shard // chunk, 2 * batches
    je, jo, others = rows_e * q, rows_o * q, max(peers - 1, 1)
    parts, sides = buffers_of(je, step_of(rows_e) * q, lax.axis_size("col"), batches)
    hbm = pl.BlockSpec(memory_space=pltpu.HBM)
    smem = pl.BlockSpec(memory_space=pltpu.SMEM)
    vmem = pl.BlockSpec(memory_space=pltpu.VMEM)
    dma = lambda *shape: pltpu.SemaphoreType.DMA(shape)
    piece = (width, chunk)
    out = jax.ShapeDtypeStruct((1, batches, shard, width), F32)
    scratch = [
        pltpu.VMEM((rows_e, cols_e, tile, twice), BF16),
        pltpu.VMEM((rows_e, cols_e, tile, twice), BF16),
        pltpu.VMEM((rows_o, cols_o, tile, twice), BF16),
        pltpu.VMEM((rows_o, cols_o, tile, twice), BF16),
        pltpu.VMEM((2, batches, shard, width), F32),
        pltpu.VMEM((2, batches, shard, width), F32),
        pltpu.VMEM((sides, je) + piece, BF16),
        pltpu.VMEM((sides, je) + piece, BF16),
        pltpu.VMEM((je,) + piece, BF16),
        pltpu.VMEM((je,) + piece, BF16),
        pltpu.VMEM((parts, je) + piece, F32),
        pltpu.VMEM((step_of(cols_o) * q,) + piece, BF16),
        pltpu.VMEM((batches, je) + piece, BF16),
        pltpu.VMEM((je,) + piece, BF16),
        pltpu.VMEM((2, batches, jo) + piece, BF16),
        pltpu.VMEM((2, rows_o, cols_o, width, twice), BF16),
        pltpu.VMEM((own,) + piece, F32),
        pltpu.VMEM((jo,) + piece, BF16),
        pltpu.VMEM((stages, others, own) + piece, BF16),
        pltpu.VMEM((own,) + piece, BF16),
        dma(2, rows_e // step_of(rows_e)),
        dma(cols_o // step_of(cols_o)),
        dma(rows_o // step_of(rows_o)),
        dma(2, 2, batches),
        dma(je),
        dma(je),
        dma(sides, je),
        dma(sides, je),
        dma(je),
        dma(batches, je),
        dma(own),
        dma(batches, own),
        dma(others, own),
        dma(stages, others, own),
        dma(jo),
        dma(stages, others, own),
    ]
    return pl.pallas_call(
        sweep_kernel,
        out_shape=[out, out],
        in_specs=[smem] * 2 + [hbm] * 6,
        out_specs=[vmem] * 2,
        scratch_shapes=scratch,
        compiler_params=pltpu.CompilerParams(
            collective_id=0,
            has_side_effects=True,
            vmem_limit_bytes=63 * 1024 * 1024,
        ),
        name="sweep",
    )(
        even_ranks.reshape(-1),
        odd_ranks.reshape(-1),
        even_left,
        even_right,
        odd_left,
        odd_right,
        even_sources,
        odd_sources,
    )


def solution(mesh):
    in_specs = (
        P(None, "layer", "row", "col", None, None),
        P(None, "layer", "row", "col", None, None),
        P(None, "layer", "col", "row", None, None),
        P(None, "layer", "col", "row", None, None),
        P(None, "layer", "row", "col"),
        P(None, "layer", "col", "row"),
        P(None, "layer", None, ("row", "col"), None),
        P(None, "layer", None, ("col", "row"), None),
    )
    out_specs = (P("layer", None, ("row", "col"), None), P("layer", None, ("col", "row"), None))
    return jax.shard_map(
        on_device, mesh=mesh, in_specs=in_specs, out_specs=out_specs, check_vma=False
    )
```

```python
import functools

import jax
import jax.numpy as jnp
from jax import lax
from jax.experimental import pallas as pl
from jax.experimental.pallas import tpu as pltpu
from jax.sharding import PartitionSpec as P

MESH = pl.DeviceIdType.MESH
F32, BF16 = jnp.float32, jnp.bfloat16


def sizes(right, sources):
    _, _, rows, cols, tile, twice = right.shape
    batches, shard, width = sources.shape[2:]
    return rows, cols, tile, twice, batches, shard, width, min(tile, shard)


def step_of(count):
    return 2 if count % 2 == 0 else 1


def skew_of(count, line):
    return max(1, min(4, (count - 2) // max(line - 1, 1)))


def buffers_of(count, step, line, batches):
    return 1 if skew_of(count, line) * (line - 1) <= count - step else 2, 2 if batches <= 2 else 2 * batches


def sweep_kernel(
    erank, orank, eleft, eright, oleft, oright, esrc, osrc, eout, oout,
    ev, eu, ov, ou, se, so, a_recv, b_recv, a_send, b_send, part, x_local, x_odd, x_hand, x_even,
    stk, sums, acc, rs_send, rs_recv,
    le_sem, lv_sem, lu_sem, src_sem, as_sem, bs_sem, ar_sem, br_sem, us_sem, ur_sem, hs_sem, hr_sem,
    gs_sem, gr_sem, rss_sem, rsr_sem,
):
    rows_e, cols_e, tile, twice, batches, shard, width, chunk = sizes(eright, esrc)
    rows_o, cols_o = oright.shape[2:4]
    half, batch = twice // 2, width // 2
    q = tile // chunk
    own = shard // chunk
    je, jo = rows_e * q, rows_o * q
    pe, po = step_of(rows_e), step_of(cols_o)
    pr = step_of(rows_o)
    segments, peers, line = (lax.axis_size(axis) for axis in ("layer", "row", "col"))
    p, r, i = (lax.axis_index(axis) for axis in ("layer", "row", "col"))
    skew, lag, ends = skew_of(je, line), 2 * po * q, batches * je
    parts, sides = buffers_of(je, pe * q, line, batches)
    early = max(cols_o // po * 3 // 4, 1)
    first = jnp.where(2 * p <= segments - 1, 0, 1)
    has_e = lambda way: jnp.logical_or(way == 1, p > 0)
    has_o = lambda way: jnp.logical_or(way == 0, p < segments - 1)

    barrier = pltpu.get_barrier_semaphore()
    expect = jnp.int32(peers - 1)
    for k in range(1, peers):
        pl.semaphore_signal(barrier, inc=1, device_id={"row": lax.rem(r + k, peers)}, device_id_type=MESH)
    for axis, at, size in (("col", i, line), ("layer", p, segments)):
        for ok, to in ((at > 0, at - 1), (at < size - 1, at + 1)):

            @pl.when(ok)
            def _(axis=axis, to=to):
                pl.semaphore_signal(barrier, inc=1, device_id={axis: to}, device_id_type=MESH)

            expect = expect + jnp.where(ok, 1, 0)

    def src_copy(parity, way, m):
        ref, buf = ((esrc, se), (osrc, so))[parity]
        return pltpu.make_async_copy(ref.at[way, 0, m], buf.at[way, m], src_sem.at[parity, way, m])

    def load_e(way, t):
        at = pl.ds(t * pe, pe)
        return [
            pltpu.make_async_copy(ref.at[way, 0, at], buf.at[at], le_sem.at[n, t])
            for n, (ref, buf) in enumerate(((eright, ev), (eleft, eu)))
        ]

    def load_v(way, t):
        at = pl.ds(t * po, po)
        return pltpu.make_async_copy(oright.at[way, 0, :, at], ov.at[:, at], lv_sem.at[t])

    def load_u(way, t):
        at = pl.ds(t * pr, pr)
        return pltpu.make_async_copy(oleft.at[way, 0, at], ou.at[at], lu_sem.at[t])

    def load_all(which, way):
        if which == 0:

            @pl.loop(0, rows_e // pe)
            def _(t):
                for copy in load_e(way, t):
                    copy.start()

        else:

            @pl.loop(0, cols_o // po)
            def _(t):
                load_v(way, t).start()

            @pl.loop(0, rows_o // pr)
            def _(t):
                load_u(way, t).start()

    for parity in range(2):
        for way in range(2):
            for m in range(batches):
                src_copy(parity, way, m).start()
    second = 1 - first
    for turn in range(2):
        for which, has in ((0, has_e), (1, has_o)):
            now = (first == which) if turn == 0 else (first != which)

            @pl.when(now & has(first))
            def _(which=which):
                load_all(which, first)

            @pl.when(now & jnp.logical_not(has(first)) & has(second))
            def _(which=which):
                load_all(which, second)

    pl.semaphore_wait(barrier, expect)

    lane = lax.broadcasted_iota(jnp.int32, (1, twice), 1)
    sign = jnp.where(lane < half, 1.0, -1.0).astype(F32)
    within = jnp.where(lane < half, lane, lane - half)

    def stacked_of(coeff, rank):
        mask = (within < rank).astype(F32)
        top = (coeff[:batch] * sign - pltpu.roll(coeff[batch:], half, 1)) * mask
        low = pltpu.roll(top, half, 1) * (-sign)
        return jnp.concatenate([top, low], axis=0).astype(BF16)

    def tile_of(load, t):
        pieces = [load(t * q + n) for n in range(q)]
        return pieces[0] if q == 1 else jnp.concatenate(pieces, axis=1)

    def source_t(buf, way, m, t):
        return buf[way, m, pl.ds(pl.multiple_of(t * chunk, chunk), chunk), :].T

    def keep(out, turn, m, t, value):
        at = pl.ds(pl.multiple_of(t * chunk, chunk), chunk)

        @pl.when(turn == 0)
        def _():
            out[0, m, at, :] = value.T

        @pl.when(turn != 0)
        def _():
            out[0, m, at, :] = out[0, m, at, :] + value.T

    def even_product(way, m, a):
        stacked = [[] for _ in range(pe)]
        for c in range(cols_e):
            right = jnp.concatenate([ev[a + j, c] for j in range(pe)], axis=1)
            x = tile_of(lambda n: x_even[way, m, n], c)
            coeff = jnp.dot(x, right, preferred_element_type=F32)
            for j in range(pe):
                rank = erank[(way * rows_e + a + j) * cols_e + c]
                stacked[j].append(stacked_of(coeff[:, j * twice : (j + 1) * twice], rank))
        for j in range(pe):
            total = lax.dot_general(
                jnp.concatenate(stacked[j], axis=1),
                jnp.concatenate([eu[a + j, c] for c in range(cols_e)], axis=1),
                (((1,), (1,)), ((), ())),
                preferred_element_type=F32,
            )
            for n in range(q):
                part[lax.rem(m, parts), (a + j) * q + n] = total[:, n * chunk : (n + 1) * chunk]

    def contract(way, a, columns):
        return [
            lax.dot_general(
                jnp.concatenate([stk[way, a + j, c] for c in columns], axis=1),
                jnp.concatenate([ou[a + j, c] for c in columns], axis=1),
                (((1,), (1,)), ((), ())),
                preferred_element_type=F32,
            )
            for j in range(pr)
        ]

    def odd_columns(way, k, m, t, load):
        @pl.when(m == 0)
        def _():
            load_v(way, t).wait()

        for g in range(po):
            c = t * po + g
            x = tile_of(load, c)
            for a in range(0, rows_o, pr):
                right = jnp.concatenate([ov[a + j, c] for j in range(pr)], axis=1)
                coeff = jnp.dot(x, right, preferred_element_type=F32)
                for j in range(pr):
                    rank = orank[(way * rows_o + a + j) * cols_o + c]
                    stk[way, a + j, c] = stacked_of(coeff[:, j * twice : (j + 1) * twice], rank)

        @pl.when((k == batches - 1) & has_o(second))
        def _():
            load_v(second, t).start()

        @pl.when(t == early - 1)
        def _():
            @pl.loop(0, rows_o // pr)
            def _(n):
                @pl.when(m == 0)
                def _():
                    load_u(way, n).wait()

                for j, total in enumerate(contract(way, n * pr, range(early * po))):
                    for h in range(q):
                        sums[(n * pr + j) * q + h] = total[:, h * chunk : (h + 1) * chunk]

    def a_copy(k, j):
        return pltpu.make_async_remote_copy(
            src_ref=a_send.at[j], dst_ref=a_recv.at[lax.rem(k, sides), j],
            send_sem=as_sem.at[j], recv_sem=ar_sem.at[lax.rem(k, sides), j],
            device_id={"col": lax.rem(i + 1, line)}, device_id_type=MESH,
        )

    def b_copy(k, j):
        return pltpu.make_async_remote_copy(
            src_ref=b_send.at[j], dst_ref=b_recv.at[lax.rem(k, sides), j],
            send_sem=bs_sem.at[j], recv_sem=br_sem.at[lax.rem(k, sides), j],
            device_id={"col": lax.rem(i + line - 1, line)}, device_id_type=MESH,
        )

    def up_copy(m, j):
        return pltpu.make_async_remote_copy(
            src_ref=x_hand.at[j], dst_ref=x_odd.at[m, j],
            send_sem=us_sem.at[j], recv_sem=ur_sem.at[m, j],
            device_id={"layer": lax.rem(p + segments - 1, segments)}, device_id_type=MESH,
        )

    def down_copy(m, t):
        return pltpu.make_async_remote_copy(
            src_ref=rs_send.at[r * own + t], dst_ref=x_even.at[0, m, r * own + t],
            send_sem=hs_sem.at[t], recv_sem=hr_sem.at[m, t],
            device_id={"layer": lax.rem(p + 1, segments)}, device_id_type=MESH,
        )

    def gather_copy(k, way, m, t, d, source):
        slot = x_even.at[way, m, source * own + t]
        return pltpu.make_async_remote_copy(
            src_ref=slot, dst_ref=slot,
            send_sem=gs_sem.at[d - 1, t], recv_sem=gr_sem.at[k, d - 1, t],
            device_id={"row": lax.rem(r + d, peers)}, device_id_type=MESH,
        )

    def scatter_copy(k, at, d):
        return pltpu.make_async_remote_copy(
            src_ref=rs_send.at[at], dst_ref=rs_recv.at[lax.rem(k, sides), d - 1, lax.rem(at, own)],
            send_sem=rss_sem.at[at], recv_sem=rsr_sem.at[k, d - 1, lax.rem(at, own)],
            device_id={"row": lax.rem(r + d, peers)}, device_id_type=MESH,
        )

    across = (first == 0) & (2 * (p + 1) > segments - 1) & (p < segments - 1)
    behind = jnp.maximum(i, line - 1 - i)

    def sweep_pass(way, turn):
        full = has_e(way)
        final = jnp.logical_and(way == 1, p == 0)
        base = turn * batches

        def sends_a(at, o):
            need = jnp.logical_or(full, at >= o) & (jnp.logical_not(final) | (o > at))
            return need & (at >= 0) & (at < line - 1)

        def sends_b(at, o):
            need = jnp.logical_or(full, at <= o) & (jnp.logical_not(final) | (o < at))
            return need & (at > 0) & (at < line)

        def opening(m):
            k = base + m
            src_copy(0, way, m).wait()
            if way == 1:
                odd_rest(1, k, turn, m)

            @pl.when(full)
            def _():
                for t in range(own):
                    if way == 0:
                        down_copy(m, t).wait_recv()
                        for d in range(1, peers):
                            gather_copy(k, way, m, t, d, r).start()
                if way == 1:
                    keep_odd(turn, m)
                for t in range(own):
                    for d in range(1, peers):
                        gather_copy(k, way, m, t, d, lax.rem(r + peers - d, peers)).wait_recv()
                for t in range(own):
                    for d in range(1, peers):
                        gather_copy(k, way, m, t, d, r).wait_send()

        @pl.loop(0, ends + skew * (line - 1) + lag)
        def _(s):
            @pl.when(s < ends)
            def _():
                m, j = s // je, lax.rem(s, je)
                page = lax.rem(m, parts)

                @pl.when(j == 0)
                def _():
                    opening(m)

                @pl.when(full & (lax.rem(j, pe * q) == 0))
                def _():
                    t = j // (pe * q)

                    @pl.when(m == 0)
                    def _():
                        for copy in load_e(way, t):
                            copy.wait()

                    even_product(way, m, t * pe)

                    @pl.when((turn == 0) & (m == batches - 1) & has_e(second))
                    def _():
                        for copy in load_e(second, t):
                            copy.start()

                    for n in range(pe * q):
                        mine = j + n - i * own

                        @pl.when((mine >= 0) & (mine < own))
                        def _(n=n, mine=mine):
                            part[page, j + n] = part[page, j + n] + source_t(se, way, m, mine)

                @pl.when(jnp.logical_not(full))
                def _():
                    mine = j - i * own
                    part[page, j] = jnp.zeros((width, chunk), F32)

                    @pl.when((mine >= 0) & (mine < own))
                    def _():
                        part[page, j] = source_t(se, way, m, mine)

            ga = s - skew * i

            @pl.when((ga >= 0) & (ga < ends))
            def _():
                m, j = ga // je, lax.rem(ga, je)
                k, page, o = base + m, lax.rem(m, parts), j // own
                got, put = sends_a(i - 1, o), sends_a(i, o)

                @pl.when(got)
                def _():
                    a_copy(k, j).wait_recv()

                @pl.when(put & (m > 0))
                def _():
                    a_copy(k - 1, j).wait_send()

                @pl.when(put & got)
                def _():
                    a_send[j] = (part[page, j] + a_recv[lax.rem(k, sides), j].astype(F32)).astype(BF16)

                @pl.when(put & jnp.logical_not(got))
                def _():
                    a_send[j] = part[page, j].astype(BF16)

                @pl.when(put)
                def _():
                    a_copy(k, j).start()

            gb = s - skew * (line - 1 - i)

            @pl.when((gb >= 0) & (gb < ends))
            def _():
                m, j = gb // je, lax.rem(gb, je)
                k, page, o = base + m, lax.rem(m, parts), j // own
                got, put = sends_b(i + 1, o), sends_b(i, o)

                @pl.when(got)
                def _():
                    b_copy(k, j).wait_recv()

                @pl.when(put & (m > 0))
                def _():
                    b_copy(k - 1, j).wait_send()

                @pl.when(put & got)
                def _():
                    b_send[j] = (part[page, j] + b_recv[lax.rem(k, sides), j].astype(F32)).astype(BF16)

                @pl.when(put & jnp.logical_not(got))
                def _():
                    b_send[j] = part[page, j].astype(BF16)

                @pl.when(put)
                def _():
                    b_copy(k, j).start()

            gt = s - skew * behind

            @pl.when((gt >= 0) & (gt < ends))
            def _():
                m, j = gt // je, lax.rem(gt, je)
                k, page, o = base + m, lax.rem(m, parts), j // own
                mine = o == i

                @pl.when(jnp.logical_not(final) | mine)
                def _():
                    @pl.when(sends_a(i - 1, o))
                    def _():
                        part[page, j] = part[page, j] + a_recv[lax.rem(k, sides), j].astype(F32)

                    @pl.when(sends_b(i + 1, o))
                    def _():
                        part[page, j] = part[page, j] + b_recv[lax.rem(k, sides), j].astype(F32)

                if way == 1:

                    @pl.when(jnp.logical_not(final))
                    def _():
                        @pl.when(m > 0)
                        def _():
                            up_copy(m - 1, j).wait_send()

                        x_hand[j] = part[page, j].astype(BF16)
                        up_copy(m, j).start()

                @pl.when(mine)
                def _():
                    keep(eout, turn, m, j - i * own, part[page, j])

                if way == 0:

                    @pl.when(j == 0)
                    def _():
                        odd_start(0, m)

                    x_local[lax.rem(j, po * q)] = part[page, j].astype(BF16)

                    @pl.when(lax.rem(j, po * q) == po * q - 1)
                    def _():
                        odd_columns(way, k, m, j // (po * q), lambda n: x_local[lax.rem(n, po * q)])

                    @pl.when(j == je - 1)
                    def _():
                        odd_rest(0, k, turn, m)
                        keep_odd(turn, m)

                else:

                    @pl.when((j == 0) & (m < batches - 1))
                    def _():
                        odd_start(1, m + 1)

            if way == 0:
                ju = gt - lag - (batches - 1) * je

                @pl.when((turn == 0) & across & (ju >= 0) & (ju < je) & (lax.rem(ju + je, po * q) == po * q - 1))
                def _():
                    up_columns(base + batches, 0, ju // (po * q))

            else:
                j = lax.rem(s, je)

                @pl.when(has_o(1) & (s < ends - je) & (lax.rem(j, po * q) == po * q - 1))
                def _():
                    up_columns(base + s // je + 1, s // je + 1, j // (po * q))

        last = base + batches - 1

        @pl.loop(0, je)
        def _(j):
            o = j // own

            @pl.when(sends_a(i, o))
            def _():
                a_copy(last, j).wait_send()

            @pl.when(sends_b(i, o))
            def _():
                b_copy(last, j).wait_send()

            if way == 1:

                @pl.when(jnp.logical_not(final))
                def _():
                    up_copy(batches - 1, j).wait_send()

        if way == 0:

            @pl.when(p < segments - 1)
            def _():
                for t in range(own):
                    down_copy(batches - 1, t).wait_send()

    def keep_odd(turn, m):
        for t in range(own):
            keep(oout, turn, m, t, acc[t])

    def up_columns(k, m, t):
        for n in range(po * q):
            up_copy(m, t * po * q + n).wait_recv()
        odd_columns(1, k, m, t, lambda n: x_odd[m, n])

    def odd_start(way, m):
        src_copy(1, way, m).wait()
        for t in range(own):
            acc[t] = source_t(so, way, m, t)

    def odd_rest(way, k, turn, m):
        full = has_o(way)
        begin = (lax.rem(r + 1, peers) * own // (q * pr)) * pr

        @pl.when(full)
        def _():
            @pl.loop(0, rows_o // pr)
            def _(n):
                a = lax.rem(begin + n * pr, rows_o)

                rest = range(early * po, cols_o)
                totals = contract(way, a, rest) if len(rest) else [jnp.zeros((width, tile), F32)] * pr
                for j in range(pr):
                    for h in range(q):
                        at = (a + j) * q + h
                        owner = at // own
                        value = totals[j][:, h * chunk : (h + 1) * chunk] + sums[at]

                        @pl.when(owner == r)
                        def _(at=at, value=value):
                            mine = at - r * own
                            acc[mine] = acc[mine] + value

                        @pl.when(owner != r)
                        def _(at=at, owner=owner, value=value):
                            rs_send[at] = value.astype(BF16)
                            scatter_copy(k, at, lax.rem(owner + peers - r, peers)).start()

                @pl.when((k == batches - 1) & has_o(second))
                def _():
                    load_u(second, a // pr).start()

            for t in range(own):
                for d in range(1, peers):
                    scatter_copy(k, r * own + t, d).wait_recv()
                    acc[t] = acc[t] + rs_recv[lax.rem(k, sides), d - 1, t].astype(F32)

        for t in range(own):
            if way == 0:

                @pl.when(p < segments - 1)
                def _(t=t):
                    @pl.when(m > 0)
                    def _():
                        down_copy(m - 1, t).wait_send()

                    rs_send[r * own + t] = acc[t].astype(BF16)
                    down_copy(m, t).start()

            else:
                x_even[way, m, r * own + t] = acc[t].astype(BF16)
                for d in range(1, peers):
                    gather_copy(k, way, m, t, d, r).start()

        @pl.when(full)
        def _():
            @pl.loop(0, jo)
            def _(at):
                owner = at // own

                @pl.when(owner != r)
                def _():
                    scatter_copy(k, at, lax.rem(owner + peers - r, peers)).wait_send()

    @pl.loop(0, 2)
    def _(turn):
        way = jnp.where(turn == 0, first, second)

        @pl.when(way == 0)
        def _():
            sweep_pass(0, turn)

        @pl.when(way == 1)
        def _():
            odd_start(1, 0)

            @pl.when(has_o(1) & ((turn == 0) | jnp.logical_not(across)))
            def _():
                @pl.loop(0, cols_o // po)
                def _(t):
                    up_columns(turn * batches, 0, t)

            sweep_pass(1, turn)


def on_device(even_left, even_right, odd_left, odd_right, even_ranks, odd_ranks, even_sources, odd_sources):
    rows_e, cols_e, tile, twice, batches, shard, width, chunk = sizes(even_right, even_sources)
    rows_o, cols_o = odd_right.shape[2:4]
    peers = lax.axis_size("row")
    q, own, stages = tile // chunk, shard // chunk, 2 * batches
    je, jo, others = rows_e * q, rows_o * q, max(peers - 1, 1)
    parts, sides = buffers_of(je, step_of(rows_e) * q, lax.axis_size("col"), batches)
    hbm = pl.BlockSpec(memory_space=pltpu.HBM)
    smem = pl.BlockSpec(memory_space=pltpu.SMEM)
    vmem = pl.BlockSpec(memory_space=pltpu.VMEM)
    dma = lambda *shape: pltpu.SemaphoreType.DMA(shape)
    piece = (width, chunk)
    out = jax.ShapeDtypeStruct((1, batches, shard, width), F32)
    scratch = [
        pltpu.VMEM((rows_e, cols_e, tile, twice), BF16),
        pltpu.VMEM((rows_e, cols_e, tile, twice), BF16),
        pltpu.VMEM((rows_o, cols_o, tile, twice), BF16),
        pltpu.VMEM((rows_o, cols_o, tile, twice), BF16),
        pltpu.VMEM((2, batches, shard, width), F32),
        pltpu.VMEM((2, batches, shard, width), F32),
        pltpu.VMEM((sides, je) + piece, BF16),
        pltpu.VMEM((sides, je) + piece, BF16),
        pltpu.VMEM((je,) + piece, BF16),
        pltpu.VMEM((je,) + piece, BF16),
        pltpu.VMEM((parts, je) + piece, F32),
        pltpu.VMEM((step_of(cols_o) * q,) + piece, BF16),
        pltpu.VMEM((batches, je) + piece, BF16),
        pltpu.VMEM((je,) + piece, BF16),
        pltpu.VMEM((2, batches, jo) + piece, BF16),
        pltpu.VMEM((2, rows_o, cols_o, width, twice), BF16),
        pltpu.VMEM((jo,) + piece, F32),
        pltpu.VMEM((own,) + piece, F32),
        pltpu.VMEM((jo,) + piece, BF16),
        pltpu.VMEM((sides, others, own) + piece, BF16),
        dma(2, rows_e // step_of(rows_e)),
        dma(cols_o // step_of(cols_o)),
        dma(rows_o // step_of(rows_o)),
        dma(2, 2, batches),
        dma(je),
        dma(je),
        dma(sides, je),
        dma(sides, je),
        dma(je),
        dma(batches, je),
        dma(own),
        dma(batches, own),
        dma(others, own),
        dma(stages, others, own),
        dma(jo),
        dma(stages, others, own),
    ]
    return pl.pallas_call(
        sweep_kernel,
        out_shape=[out, out],
        in_specs=[smem] * 2 + [hbm] * 6,
        out_specs=[vmem] * 2,
        scratch_shapes=scratch,
        compiler_params=pltpu.CompilerParams(
            collective_id=0,
            has_side_effects=True,
            vmem_limit_bytes=67_000_320,
        ),
        name="sweep",
    )(
        even_ranks.reshape(-1),
        odd_ranks.reshape(-1),
        even_left,
        even_right,
        odd_left,
        odd_right,
        even_sources,
        odd_sources,
    )


def solution(mesh):
    in_specs = (
        P(None, "layer", "row", "col", None, None),
        P(None, "layer", "row", "col", None, None),
        P(None, "layer", "col", "row", None, None),
        P(None, "layer", "col", "row", None, None),
        P(None, "layer", "row", "col"),
        P(None, "layer", "col", "row"),
        P(None, "layer", None, ("row", "col"), None),
        P(None, "layer", None, ("col", "row"), None),
    )
    out_specs = (P("layer", None, ("row", "col"), None), P("layer", None, ("col", "row"), None))
    return jax.shard_map(
        on_device, mesh=mesh, in_specs=in_specs, out_specs=out_specs, check_vma=False
    )
```
